128 devices in a mesh: animal: 16 (over z, x_lo, core), snp: 8 (over x_hi, y).
Axes of the slice: x: 4 (x_hi: 2, x_lo: 2; x = x_hi * 2 + x_lo), y: 4, z: 4, core: 2. Of those that a mesh axis runs over, the one named last changes fastest.
Arguments:
- genotypes: int32 [32768, 8192], P('animal', 'snp'), may hold values from 0 to 2730, as said below
- allele_frequency: float32 [49152], P('snp'), may hold values from 0.05 to 0.5
- family_size: int32 [256], P('animal'), may hold values from 40 to 128, as said below
- rel_family: int32 [256], P('animal'), may hold values from 0 to 255, as said below
- rel_count: int32 [256], P('animal'), may hold values from 8 to 128, as said below
- own_block: bfloat16 [256, 128, 128], P('animal'), may hold values from -0.5 to 3
- rel_block: bfloat16 [256, 128, 128], P('animal'), may hold values from -0.5 to 0.5
- prior_solution: bfloat16 [32768, 128], P('animal'), may hold values from -6 to 6
- right_side: float32 [32768, 128], P('animal'), may hold values from -6 to 6
- step_scale: float32 [32768], P('animal'), may hold values from 0.1 to 0.3
Outputs:
- solution: float32 [32768, 128], P(('animal', 'snp'))
- residual: float32 [32768, 128], P(('animal', 'snp'))
The draws below stay inside these ranges and needn't reach their ends.
Inputs may be any that keep to these rules, and one draw needn't show every extreme that they name: `genotypes`: bits 2k and 2k + 1 of word w of a row hold the code 0, 1 or 2 of marker 6w + k, for k = 0 to 5; higher bits are zero; some word has all six codes 0 and some word all six codes 2. `family_size`: some family has all 128 slots live. `rel_family`: family f's relative family lies in the same block of 16 consecutive families as f or in one of the 3 blocks before it, and in the block exactly 3 before it for some family of every block that has one. `rel_count`: some family takes all 128 rows.
All inputs are finite; a program needn't handle non-finite values.
Results may differ from the reference program's by a relative error of at most 0.007.
Values may be sent and summed in bfloat16 or wider, within the bound.
A program may use at most 192 MiB of HBM per device.

```python
import math
import jax
import jax.numpy as jnp
from jax import lax

FAMSIZE = 128
SNPS = 49152
COLS = 128
ITERS = 2
RSPAN = 3
KIN_SPAN_UNIT = 16
FAMILIES = 256
ROWS = 32768


def variant_millesimal(key):
    return jax.random.randint(jax.random.fold_in(key, 11), (SNPS,), 50, 501)


def draw_allele_frequency(key, part):
    return variant_millesimal(key).astype(jnp.float32) / 1000.0


def draw_genotypes(key, part):
    millesimal_scale = variant_millesimal(key)
    twin_copy_indicator = millesimal_scale * millesimal_scale
    bears_variant_indicator = twin_copy_indicator + 2 * millesimal_scale * (1000 - millesimal_scale)
    code_key = jax.random.fold_in(key, 12)

    def one_family(family_index):
        flat_random_draws = jax.random.randint(jax.random.fold_in(code_key, family_index), (FAMSIZE, SNPS), 0, 1000000)
        dosage_states = (flat_random_draws < bears_variant_indicator[None, :]).astype(jnp.int32) + (flat_random_draws < twin_copy_indicator[None, :]).astype(jnp.int32)
        grouped = dosage_states.reshape(FAMSIZE, SNPS // 6, 6)
        packed = jnp.zeros((FAMSIZE, SNPS // 6), jnp.int32)
        for position in range(6):
            packed = jnp.bitwise_or(packed, jnp.left_shift(grouped[:, :, position], jnp.int32(2 * position)))
        return packed
    blocks = lax.map(one_family, jnp.arange(FAMILIES, dtype=jnp.int32))
    words = blocks.reshape(ROWS, SNPS // 6)
    low_row = jax.random.randint(jax.random.fold_in(key, 13), (), 0, ROWS)
    low_col = jax.random.randint(jax.random.fold_in(key, 14), (), 0, SNPS // 6)
    high_row = jax.random.randint(jax.random.fold_in(key, 15), (), 0, ROWS)
    high_col = jax.random.randint(jax.random.fold_in(key, 16), (), 0, SNPS // 6)
    high_col = jnp.where((high_row == low_row) & (high_col == low_col), (low_col + 1) % (SNPS // 6), high_col)
    words = words.at[low_row, low_col].set(jnp.int32(0))
    words = words.at[high_row, high_col].set(jnp.int32(2730))
    return words


def draw_family_size(key, part):
    sizes = jax.random.randint(jax.random.fold_in(key, 21), (FAMILIES,), FAMSIZE * 5 // 16, FAMSIZE + 1)
    full_family = jax.random.randint(jax.random.fold_in(key, 22), (), 0, FAMILIES)
    return sizes.at[full_family].set(FAMSIZE).astype(jnp.int32)


def draw_rel_family(key, part):
    family_index = jnp.arange(FAMILIES, dtype=jnp.int32)
    device_index = family_index // KIN_SPAN_UNIT
    distance = jax.random.randint(jax.random.fold_in(key, 31), (FAMILIES,), 0, RSPAN + 1)
    chosen = jax.random.randint(jax.random.fold_in(key, 32), (FAMILIES // KIN_SPAN_UNIT,), 0, KIN_SPAN_UNIT)
    distance = jnp.where(family_index % KIN_SPAN_UNIT == chosen[device_index], RSPAN, distance)
    distance = jnp.minimum(distance, device_index)
    within = jax.random.randint(jax.random.fold_in(key, 33), (FAMILIES,), 0, KIN_SPAN_UNIT)
    return ((device_index - distance) * KIN_SPAN_UNIT + within).astype(jnp.int32)


def draw_rel_count(key, part):
    counts = jax.random.randint(jax.random.fold_in(key, 35), (FAMILIES,), FAMSIZE // 16, FAMSIZE + 1)
    full_family = jax.random.randint(jax.random.fold_in(key, 36), (), 0, FAMILIES)
    return counts.at[full_family].set(FAMSIZE).astype(jnp.int32)


def draw_own_block(key, part):
    noise = jax.random.normal(jax.random.fold_in(key, 41), (FAMILIES, FAMSIZE, FAMSIZE), jnp.float32)
    diagonal = jax.random.uniform(jax.random.fold_in(key, 42), (FAMILIES, FAMSIZE), jnp.float32, 1.5, 2.5)
    identity = jnp.eye(FAMSIZE, dtype=jnp.float32)
    offdiag = noise * (0.5 / math.sqrt(FAMSIZE)) * (1.0 - identity)[None, :, :]
    return (offdiag + identity[None, :, :] * diagonal[:, None, :]).astype(jnp.bfloat16)


def levels(key, dims, split, least, high):
    factor_of, own = 1.0, jax.random.fold_in(key, 6)
    for dim, parts in split:
        draws = jnp.exp(jax.random.uniform(jax.random.fold_in(own, dim), (parts,), jnp.float32, least / len(split), high / len(split)))
        factor_of = factor_of * jnp.repeat(draws, dims[dim] // parts).reshape([-1 if axis == dim else 1 for axis in range(len(dims))])
    return factor_of


def scatter_about(rng, shape, spread, reach, split=(), kind=jnp.bfloat16):
    level = levels(rng, shape, split, -0.22, 0.18) if split else 1.0
    array = jax.random.normal(rng, shape, jnp.float32) * spread * level
    return jnp.minimum(jnp.maximum(array, -reach), reach).astype(kind)


def setup_inputs(seed: int = 0) -> dict:
    streams_of = jax.random.split(jax.random.key(seed), 11)
    return {
        "genotypes": draw_genotypes(jax.random.fold_in(streams_of[10], 71), 0),
        "allele_frequency": draw_allele_frequency(jax.random.fold_in(streams_of[10], 71), 0),
        "family_size": draw_family_size(jax.random.fold_in(streams_of[10], 71), 0),
        "rel_family": draw_rel_family(jax.random.fold_in(streams_of[10], 71), 0),
        "rel_count": draw_rel_count(jax.random.fold_in(streams_of[10], 71), 0),
        "own_block": draw_own_block(jax.random.fold_in(streams_of[10], 71), 0),
        "rel_block": scatter_about(streams_of[6], (FAMILIES, FAMSIZE, FAMSIZE), FAMSIZE ** -0.5, 0.5, ((0, 16),)),
        "prior_solution": scatter_about(streams_of[7], (ROWS, COLS), 1.0, 6.0, ((0, 16),)),
        "right_side": scatter_about(streams_of[8], (ROWS, COLS), 1.0, 6.0, ((0, 16),), jnp.float32),
        "step_scale": jnp.clip(jnp.exp(math.log(0.3) - 1.0986123 * jax.random.uniform(streams_of[9], (ROWS,), jnp.float32) ** levels(streams_of[9], (ROWS,), ((0, 16),), -0.2, 0.2)), 0.1, 0.3),
    }


GEN_WEIGHT = 6.0


def decode_rows(genotypes, allele_frequency, live_rows):
    bit_shifts = 2 * jnp.arange(6, dtype=jnp.int32)
    dosage_states = jnp.bitwise_and(jnp.right_shift(genotypes[:, :, None], bit_shifts[None, None, :]), 3)
    dosage_states = dosage_states.reshape(genotypes.shape[0], genotypes.shape[1] * 6).astype(jnp.float32)
    centered = (dosage_states - 2.0 * allele_frequency[None, :]) * live_rows[:, None]
    return centered.astype(jnp.bfloat16)


def reference(genotypes, allele_frequency, family_size, rel_family, rel_count, own_block, rel_block, prior_solution, right_side, step_scale):
    slot_index = jnp.arange(FAMSIZE, dtype=jnp.int32)
    live_rows = (slot_index[None, :] < family_size[:, None]).astype(jnp.float32).reshape(-1)
    packed_blocks = genotypes.reshape(FAMILIES, FAMSIZE, SNPS // 6)
    live_blocks = live_rows.reshape(FAMILIES, FAMSIZE)
    keep_rows = slot_index[None, :, None] < rel_count[:, None, None]
    solution_now = live_rows[:, None] * prior_solution.astype(jnp.float32)
    residual = jnp.zeros((ROWS, COLS), jnp.float32)
    for iteration in range(ITERS):
        solution_half = solution_now.astype(jnp.bfloat16)
        half_blocks = solution_half.reshape(FAMILIES, FAMSIZE, COLS)

        def add_block(running, inputs):
            packed, live_part, half_part = inputs
            centered = decode_rows(packed, allele_frequency, live_part)
            product = lax.dot_general(centered, half_part, (((0,), (0,)), ((), ())), preferred_element_type=jnp.float32)
            return running + product, 0

        snp_sum = lax.scan(add_block, jnp.zeros((SNPS, COLS), jnp.float32), (packed_blocks, live_blocks, half_blocks))[0]
        snp_half = snp_sum.astype(jnp.bfloat16)

        def genomic_block(inputs):
            packed, live_part = inputs
            return jnp.dot(decode_rows(packed, allele_frequency, live_part), snp_half, preferred_element_type=jnp.float32)

        genomic = lax.map(genomic_block, (packed_blocks, live_blocks)).reshape(ROWS, COLS)
        family_half = solution_half.reshape(FAMILIES, FAMSIZE, COLS)
        relatives = jnp.where(keep_rows, family_half[rel_family], jnp.zeros_like(family_half))
        pedigree = jnp.einsum("fij,fjk->fik", own_block.astype(jnp.float32), family_half.astype(jnp.float32))
        pedigree = pedigree + jnp.einsum("fij,fjk->fik", rel_block.astype(jnp.float32), relatives.astype(jnp.float32))
        pedigree = pedigree.reshape(ROWS, COLS)
        residual = live_rows[:, None] * (right_side - solution_now - (GEN_WEIGHT / SNPS) * genomic - pedigree)
        solution_now = solution_now + step_scale[:, None] * residual
    return solution_now, residual
```

```python
import jax
import jax.numpy as jnp
from jax import lax
from jax.experimental import pallas as pl
from jax.experimental.pallas import tpu as pltpu
from jax.sharding import PartitionSpec as P

SNPS = 49152
ITERS = 2
RSPAN = 3
GEN_WEIGHT = 6.0
PLANES = 6
FAM = 128
COLS = 128
ANIMAL = 16
SNP = 8
CHIPS = 8
ROWS = 2048
WORDS = 1024
FAMS = 16
SHARE = 256
HALF = 512
BAND = 16
ROW_BLOCKS = 8

F32 = jnp.float32
BF16 = jnp.bfloat16


def dot(a, b, ca, cb):
    return lax.dot_general(a, b, (((ca,), (cb,)), ((), ())), preferred_element_type=F32)


def remote(src, dst, send, recv, where):
    return pltpu.make_async_remote_copy(
        src_ref=src,
        dst_ref=dst,
        send_sem=send,
        recv_sem=recv,
        device_id=where,
        device_id_type=pl.DeviceIdType.MESH,
    )


def arrived(ref, sem):
    pltpu.make_async_copy(ref, ref, sem).wait()


def kernel(
    geno,
    twice_freq,
    family_size,
    rel_family,
    rel_vector,
    rel_count,
    own_block,
    rel_block,
    prior,
    right_side,
    step_scale,
    out_solution,
    out_residual,
    words,
    codes,
    half_first,
    half_second,
    both,
    core_send,
    core_recv,
    chip_send,
    chip_recv,
    whole,
    total,
    gen_send,
    gen_recv,
    share_now,
    own_now,
    couple_now,
    right_now,
    rel_send,
    rel_first,
    rel_second,
    request,
    request_scalar,
    word_sem,
    local_sem,
    request_sem,
    core_sem,
    chip_sem,
    back_sem,
    join_sem,
    gen_sem,
    half_sem,
    rel_sem,
):
    animal = lax.axis_index("animal")
    snp = lax.axis_index("snp")
    core = lax.rem(animal, 2)
    chip = animal // 2
    partner = {"animal": animal + 1 - 2 * core}

    for block in range(ROW_BLOCKS):
        rows = pl.ds(block * (ROWS // ROW_BLOCKS), ROWS // ROW_BLOCKS)
        pltpu.make_async_copy(geno.at[rows], words.at[rows], word_sem.at[block]).start()
    family_first = snp * 2
    locals_ = [
        pltpu.make_async_copy(own_block.at[pl.ds(family_first, 2)], own_now, local_sem.at[0]),
        pltpu.make_async_copy(rel_block.at[pl.ds(family_first, 2)], couple_now, local_sem.at[1]),
        pltpu.make_async_copy(right_side.at[pl.ds(snp * SHARE, SHARE)], right_now, local_sem.at[2]),
    ]
    for copy in locals_:
        copy.start()
    halves = (half_first, half_second)
    rel_recv = (rel_first, rel_second)
    for ref in rel_recv:
        ref[...] = jnp.zeros_like(ref)

    barrier = pltpu.get_barrier_semaphore()
    for step in range(1, ANIMAL):
        pl.semaphore_signal(
            barrier,
            inc=1,
            device_id={"animal": lax.rem(animal + step, ANIMAL)},
            device_id_type=pl.DeviceIdType.MESH,
        )
    for step in range(1, SNP):
        pl.semaphore_signal(
            barrier,
            inc=1,
            device_id={"snp": lax.rem(snp + step, SNP)},
            device_id_type=pl.DeviceIdType.MESH,
        )

    lane_slot = lax.broadcasted_iota(jnp.int32, (COLS, FAM), 1)
    row_slot = lax.broadcasted_iota(jnp.int32, (FAM, COLS), 0)

    def first_half(f, carry):
        block = prior[pl.ds(pl.multiple_of(f * FAM, FAM), FAM), :]
        turned = block.astype(F32).T
        halves[0][f] = jnp.where(lane_slot < family_size[f], turned, 0.0).astype(BF16)
        return carry

    lax.fori_loop(0, FAMS, first_half, 0)
    live = [
        jnp.where(row_slot < family_size[family_first + i], 1.0, 0.0).astype(F32) for i in range(2)
    ]
    for i in range(2):
        block = prior[pl.ds(pl.multiple_of((family_first + i) * FAM, FAM), FAM), :]
        share_now[i] = live[i] * block.astype(F32)

    pl.semaphore_wait(barrier, ANIMAL - 1 + SNP - 1)

    for d in range(1, RSPAN + 1):

        @pl.when(animal >= d)
        def _():
            remote(
                rel_vector,
                request.at[d - 1],
                request_sem.at[0, d - 1],
                request_sem.at[1, d - 1],
                {"animal": animal - d},
            ).start()

    def decode_block(block, carry):
        rows = pl.ds(pl.multiple_of(block * (ROWS // ROW_BLOCKS), FAM), ROWS // ROW_BLOCKS)
        pltpu.make_async_copy(geno.at[rows], words.at[rows], word_sem.at[block]).wait()

        def decode(i, inner):
            at = pl.ds(pl.multiple_of(block * (ROWS // ROW_BLOCKS) + i * 16, 16), 16)
            word = words[at, :]
            for k in range(PLANES):
                codes[k, at, :] = ((word >> (2 * k)) & 3).astype(F32).astype(BF16)
            return inner

        return lax.fori_loop(0, ROWS // ROW_BLOCKS // 16, decode, carry)

    lax.fori_loop(0, ROW_BLOCKS, decode_block, 0)

    for d in range(1, RSPAN + 1):

        @pl.when(animal + d < ANIMAL)
        def _():
            arrived(request.at[d - 1], request_sem.at[1, d - 1])
            copy = pltpu.make_async_copy(
                request.at[d - 1], request_scalar.at[d - 1], local_sem.at[3]
            )
            copy.start()
            copy.wait()

    for copy in locals_:
        copy.wait()

    for it in range(ITERS):
        for d in range(1, RSPAN + 1):

            @pl.when(animal + d < ANIMAL)
            def _():
                for i in range(2):
                    wanted = lax.rem(request_scalar[d - 1, 0, family_first + i], FAMS)
                    rel_send[it, d - 1, i] = halves[it][wanted]
                remote(
                    rel_send.at[it, d - 1],
                    rel_recv[it].at[d - 1],
                    rel_sem.at[it, 0, d - 1],
                    rel_sem.at[it, 1, d - 1],
                    {"animal": animal + d},
                ).start()

        column_sum = jnp.zeros((COLS, FAM), F32)
        for f in range(FAMS):
            column_sum = column_sum + halves[it][f].astype(F32)
        column_sum = jnp.sum(column_sum, axis=1, keepdims=True)

        total[...] = jnp.zeros_like(total)

        def to_markers(k):
            turned = jnp.concatenate([halves[it][f] for f in range(FAMS)], axis=1)
            product = dot(turned, codes[k], 1, 0) - column_sum * twice_freq[k]
            both[k, 0] = product[:, :HALF]
            both[k, 1] = product[:, HALF:]
            core_send[it, k] = both[k, 1 - core].astype(BF16).reshape(CHIPS, BAND, HALF)
            remote(
                core_send.at[it, k],
                core_recv.at[it, k],
                core_sem.at[it, 0, k],
                core_sem.at[it, 1, k],
                partner,
            ).start()

        def over_chips(k):
            arrived(core_recv.at[it, k], core_sem.at[it, 1, k])
            summed = both[k, core].reshape(CHIPS, BAND, HALF) + core_recv[it, k].astype(F32)
            both[k, core] = summed.reshape(COLS, HALF)
            chip_send[it, k] = summed.astype(BF16)
            for d in range(1, CHIPS):
                to = lax.rem(chip + d, CHIPS)
                remote(
                    chip_send.at[it, k, to],
                    chip_recv.at[it, k, CHIPS - 1 - d],
                    chip_sem.at[it, 0, k],
                    chip_sem.at[it, 1, k],
                    {"animal": to * 2 + core},
                ).start()

        def to_chips(k):
            arrived(chip_recv.at[it, k], chip_sem.at[it, 1, k])
            mine = both[k, core, pl.ds(pl.multiple_of(chip * BAND, BAND), BAND), :]
            for d in range(CHIPS - 1):
                mine = mine + chip_recv[it, k, d].astype(F32)
            whole[it, k, core, chip] = mine.astype(BF16)
            for d in range(1, CHIPS):
                to = lax.rem(chip + d, CHIPS)
                remote(
                    whole.at[it, k, core, chip],
                    whole.at[it, k, core, chip],
                    back_sem.at[it, 0, k],
                    back_sem.at[it, 1, k],
                    {"animal": to * 2 + core},
                ).start()

        def to_core(k):
            arrived(chip_recv.at[it, k], back_sem.at[it, 1, k])
            remote(
                whole.at[it, k, core],
                whole.at[it, k, core],
                join_sem.at[it, 0, k],
                join_sem.at[it, 1, k],
                partner,
            ).start()

        def to_animals(k, shift):
            arrived(core_recv.at[it, k], join_sem.at[it, 1, k])
            lower = whole[it, k, 0].reshape(COLS, HALF)
            upper = whole[it, k, 1].reshape(COLS, HALF)
            sums = jnp.concatenate([lower, upper], axis=1)
            total[...] += dot(codes[k], sums, 1, 1)
            weighed = sums.astype(F32) * twice_freq[k]
            return shift + jnp.sum(weighed, axis=1, keepdims=True)

        def step(t, shift):
            for stage, offset in ((to_core, 3), (to_chips, 2), (over_chips, 1), (to_markers, 0)):
                k = t - offset

                @pl.when((k >= 0) & (k < PLANES))
                def _():
                    stage(k)

            k = t - 4
            return lax.cond(k >= 0, lambda s: to_animals(k, s), lambda s: s, shift)

        shift = lax.fori_loop(0, PLANES + 4, step, jnp.zeros((COLS, 1), F32))
        shift = jnp.broadcast_to(shift, (COLS, COLS)).T[:1]

        for d in range(1, SNP):
            to = lax.rem(snp + d, SNP)
            rows = pl.ds(pl.multiple_of(to * SHARE, SHARE), SHARE)
            gen_send[it, d - 1] = (total[rows, :] - shift).astype(BF16)
            remote(
                gen_send.at[it, d - 1],
                gen_recv.at[it, d - 1],
                gen_sem.at[it, 0],
                gen_sem.at[it, 1],
                {"snp": to},
            ).start()

        for d in range(1, RSPAN + 1):

            @pl.when(animal >= d)
            def _():
                arrived(rel_recv[it].at[d - 1], rel_sem.at[it, 1, d - 1])

        pedigree = []
        for i in range(2):
            family = family_first + i
            relative = rel_family[family]
            distance = animal - relative // FAMS
            here = halves[it][lax.rem(relative, FAMS)]
            there = rel_recv[it][jnp.clip(distance - 1, 0, RSPAN - 1), i]
            taken = jnp.where(distance == 0, here.astype(F32), there.astype(F32))
            taken = jnp.where(lane_slot < rel_count[family], taken, 0.0).astype(BF16)
            pedigree.append(
                dot(own_now[i], halves[it][family], 1, 1) + dot(couple_now[i], taken, 1, 1)
            )

        arrived(gen_recv.at[it], gen_sem.at[it, 1])
        for i in range(2):
            own_rows = pl.ds(pl.multiple_of(snp * SHARE + i * FAM, FAM), FAM)
            genomic = total[own_rows, :] - shift
            for d in range(SNP - 1):
                genomic = genomic + gen_recv[it, d, pl.ds(i * FAM, FAM), :].astype(F32)
            residual = live[i] * (
                right_now[pl.ds(i * FAM, FAM), :]
                - share_now[i]
                - GEN_WEIGHT / SNPS * genomic
                - pedigree[i]
            )
            scale = jnp.broadcast_to(step_scale[pl.ds(family_first + i, 1), :], (FAM, FAM)).T
            updated = share_now[i] + scale * residual
            if it + 1 < ITERS:
                share_now[i] = updated
                halves[it + 1][family_first + i] = updated.T.astype(BF16)
            else:
                out_solution[pl.ds(i * FAM, FAM), :] = updated
                out_residual[pl.ds(i * FAM, FAM), :] = residual

        if it + 1 < ITERS:
            mine = halves[it + 1].at[pl.ds(family_first, 2)]
            for d in range(1, SNP):
                remote(
                    mine,
                    mine,
                    half_sem.at[0],
                    half_sem.at[1],
                    {"snp": lax.rem(snp + d, SNP)},
                ).start()
            arrived(halves[it + 1].at[pl.ds(0, 14)], half_sem.at[1])

    arrived(halves[1].at[pl.ds(0, 14)], half_sem.at[0])
    for d in range(1, RSPAN + 1):

        @pl.when(animal >= d)
        def _():
            arrived(rel_vector, request_sem.at[0, d - 1])

        @pl.when(animal + d < ANIMAL)
        def _():
            for it in range(ITERS):
                arrived(rel_send.at[it, d - 1], rel_sem.at[it, 0, d - 1])

    for it in range(ITERS):
        arrived(gen_send.at[it], gen_sem.at[it, 0])

        def sent(k, carry):
            arrived(core_send.at[it, k], core_sem.at[it, 0, k])
            arrived(core_send.at[it, k], join_sem.at[it, 0, k])
            arrived(chip_recv.at[it, k], chip_sem.at[it, 0, k])
            arrived(chip_recv.at[it, k], back_sem.at[it, 0, k])
            return carry

        lax.fori_loop(0, PLANES, sent, 0)


def per_device(
    genotypes,
    allele_frequency,
    family_size,
    rel_family,
    rel_count,
    own_block,
    rel_block,
    prior_solution,
    right_side,
    step_scale,
):
    twice_freq = (2.0 * allele_frequency).reshape(WORDS, PLANES).T.reshape(PLANES, 1, WORDS)
    vmem = pl.BlockSpec(memory_space=pltpu.VMEM)
    smem = pl.BlockSpec(memory_space=pltpu.SMEM)
    hbm = pl.BlockSpec(memory_space=pl.ANY)
    dma = pltpu.SemaphoreType.DMA
    share = jax.ShapeDtypeStruct((SHARE, COLS), F32)
    rel_vector = jnp.pad(rel_family, (0, 128 - FAMS)).reshape(1, 128)
    return pl.pallas_call(
        kernel,
        out_shape=(share, share),
        in_specs=[hbm, vmem, smem, smem, vmem, smem, hbm, hbm, vmem, hbm, vmem],
        out_specs=(vmem, vmem),
        scratch_shapes=[
            pltpu.VMEM((ROWS, WORDS), jnp.int32),
            pltpu.VMEM((PLANES, ROWS, WORDS), BF16),
            pltpu.VMEM((FAMS, COLS, FAM), BF16),
            pltpu.VMEM((FAMS, COLS, FAM), BF16),
            pltpu.VMEM((PLANES, 2, COLS, HALF), F32),
            pltpu.VMEM((ITERS, PLANES, CHIPS, BAND, HALF), BF16),
            pltpu.VMEM((ITERS, PLANES, CHIPS, BAND, HALF), BF16),
            pltpu.VMEM((ITERS, PLANES, CHIPS, BAND, HALF), BF16),
            pltpu.VMEM((ITERS, PLANES, CHIPS - 1, BAND, HALF), BF16),
            pltpu.VMEM((ITERS, PLANES, 2, CHIPS, BAND, HALF), BF16),
            pltpu.VMEM((ROWS, COLS), F32),
            pltpu.VMEM((ITERS, SNP - 1, SHARE, COLS), BF16),
            pltpu.VMEM((ITERS, SNP - 1, SHARE, COLS), BF16),
            pltpu.VMEM((2, FAM, COLS), F32),
            pltpu.VMEM((2, FAM, FAM), BF16),
            pltpu.VMEM((2, FAM, FAM), BF16),
            pltpu.VMEM((SHARE, COLS), F32),
            pltpu.VMEM((ITERS, RSPAN, 2, COLS, FAM), BF16),
            pltpu.VMEM((RSPAN, 2, COLS, FAM), BF16),
            pltpu.VMEM((RSPAN, 2, COLS, FAM), BF16),
            pltpu.VMEM((RSPAN, 1, 128), jnp.int32),
            pltpu.SMEM((RSPAN, 1, 128), jnp.int32),
            dma((ROW_BLOCKS,)),
            dma((4,)),
            dma((2, RSPAN)),
            dma((ITERS, 2, PLANES)),
            dma((ITERS, 2, PLANES)),
            dma((ITERS, 2, PLANES)),
            dma((ITERS, 2, PLANES)),
            dma((ITERS, 2)),
            dma((2,)),
            dma((ITERS, 2, RSPAN)),
        ],
        compiler_params=pltpu.CompilerParams(
            collective_id=0, has_side_effects=True, vmem_limit_bytes=66 * 10**6
        ),
        name="blup",
    )(
        genotypes,
        twice_freq,
        family_size,
        rel_family,
        rel_vector,
        rel_count,
        own_block,
        rel_block,
        prior_solution,
        right_side,
        step_scale.reshape(FAMS, FAM),
    )


def solution(mesh):
    in_specs = (
        P("animal", "snp"),
        P("snp"),
        P("animal"),
        P("animal"),
        P("animal"),
        P("animal", None, None),
        P("animal", None, None),
        P("animal", None),
        P("animal", None),
        P("animal"),
    )
    out_specs = (P(("animal", "snp"), None), P(("animal", "snp"), None))
    return jax.shard_map(
        per_device, mesh=mesh, in_specs=in_specs, out_specs=out_specs, check_vma=False
    )
```

```python
import jax
import jax.numpy as jnp
from jax import lax
from jax.experimental import pallas as pl
from jax.experimental.pallas import tpu as pltpu
from jax.sharding import PartitionSpec as P

SNPS = 49152
ITERS = 2
RSPAN = 3
GEN_WEIGHT = 6.0
PLANES = 6
FAM = 128
COLS = 128
ANIMAL = 16
SNP = 8
CHIPS = 8
ROWS = 2048
WORDS = 1024
FAMS = 16
SHARE = 256
HALF = 512
BAND = 16
ROW_BLOCKS = 8

F32 = jnp.float32
BF16 = jnp.bfloat16


def dot(a, b, ca, cb):
    return lax.dot_general(a, b, (((ca,), (cb,)), ((), ())), preferred_element_type=F32)


def remote(src, dst, send, recv, where):
    return pltpu.make_async_remote_copy(
        src_ref=src,
        dst_ref=dst,
        send_sem=send,
        recv_sem=recv,
        device_id=where,
        device_id_type=pl.DeviceIdType.MESH,
    )


def arrived(ref, sem):
    pltpu.make_async_copy(ref, ref, sem).wait()


def kernel(
    geno,
    freq,
    family_size,
    rel_family,
    rel_vector,
    rel_count,
    own_block,
    rel_block,
    prior,
    right_side,
    step_scale,
    out,
    words,
    codes,
    half_first,
    half_second,
    both,
    core_send,
    core_recv,
    chip_send,
    chip_recv,
    whole,
    total,
    gen_send,
    gen_recv,
    share_now,
    own_now,
    couple_now,
    right_now,
    rel_send,
    rel_first,
    rel_second,
    request_one,
    request_two,
    request_three,
    scalar_one,
    scalar_two,
    scalar_three,
    twice_freq,
    word_sem,
    local_sem,
    request_sem,
    core_sem,
    chip_sem,
    back_sem,
    join_sem,
    gen_sem,
    half_sem,
    rel_sem,
):
    animal = lax.axis_index("animal")
    snp = lax.axis_index("snp")
    core = lax.rem(animal, 2)
    chip = animal // 2
    request = (request_one, request_two, request_three)
    request_scalar = (scalar_one, scalar_two, scalar_three)
    partner = {"animal": animal + 1 - 2 * core}
    other_chips = [
        lax.rem(chip // 2 + dz, 4) * 2 + lax.rem(lax.rem(chip, 2) + dx, 2)
        for dz, dx in ((2, 1), (1, 1), (3, 1), (2, 0), (1, 0), (3, 0), (0, 1))
    ]

    def peer(step):
        far = 1 - step // 4
        return lax.rem(snp // 4 + far, 2) * 4 + lax.rem(lax.rem(snp, 4) + 3 - lax.rem(step, 4), 4)


    for block in range(ROW_BLOCKS):
        rows = pl.ds(block * (ROWS // ROW_BLOCKS), ROWS // ROW_BLOCKS)
        pltpu.make_async_copy(geno.at[rows], words.at[rows], word_sem.at[block]).start()
    family_first = snp * 2
    locals_ = [
        pltpu.make_async_copy(own_block.at[pl.ds(family_first, 2)], own_now, local_sem.at[0]),
        pltpu.make_async_copy(rel_block.at[pl.ds(family_first, 2)], couple_now, local_sem.at[1]),
        pltpu.make_async_copy(right_side.at[pl.ds(snp * SHARE, SHARE)], right_now, local_sem.at[2]),
    ]
    for copy in locals_:
        copy.start()
    halves = (half_first, half_second)
    rel_recv = (rel_first, rel_second)
    for ref in rel_recv:
        ref[...] = jnp.zeros_like(ref)

    barrier = pltpu.get_barrier_semaphore()
    for step in range(1, ANIMAL):
        pl.semaphore_signal(
            barrier,
            inc=1,
            device_id={"animal": lax.rem(animal + step, ANIMAL)},
            device_id_type=pl.DeviceIdType.MESH,
        )
    for step in range(1, SNP):
        pl.semaphore_signal(
            barrier,
            inc=1,
            device_id={"snp": lax.rem(snp + step, SNP)},
            device_id_type=pl.DeviceIdType.MESH,
        )

    lane_slot = lax.broadcasted_iota(jnp.int32, (COLS, FAM), 1)
    row_slot = lax.broadcasted_iota(jnp.int32, (FAM, COLS), 0)

    def first_half(f, carry):
        block = prior[pl.ds(pl.multiple_of(f * FAM, FAM), FAM), :]
        turned = block.astype(F32).T
        halves[0][f] = jnp.where(lane_slot < family_size[f], turned, 0.0).astype(BF16)
        return carry

    lax.fori_loop(0, FAMS, first_half, 0)
    live = [
        jnp.where(row_slot < family_size[family_first + i], 1.0, 0.0).astype(F32) for i in range(2)
    ]
    for i in range(2):
        block = prior[pl.ds(pl.multiple_of((family_first + i) * FAM, FAM), FAM), :]
        share_now[i] = live[i] * block.astype(F32)

    lane = lax.broadcasted_iota(jnp.int32, (128, PLANES * 128), 0)
    column = lax.broadcasted_iota(jnp.int32, (128, PLANES * 128), 1)
    marker = PLANES * (column & 127) + (column >> 7)
    by_plane = jnp.zeros((24, PLANES * 128), F32)
    for r in range(PLANES):
        rest = 2.0 * freq[pl.ds(r, 8, stride=PLANES), :]
        parts = []
        for _ in range(3):
            part = rest.astype(BF16).astype(F32)
            parts.append(part)
            rest = rest - part
        chosen = jnp.where(marker == lane + 128 * r, 1.0, 0.0).astype(BF16)
        by_plane = by_plane + dot(jnp.concatenate(parts, axis=0).astype(BF16), chosen, 1, 0)
    by_plane = by_plane[:8] + by_plane[8:16] + by_plane[16:]
    for k in range(PLANES):
        for q in range(8):
            twice_freq[k, :, pl.ds(q * 128, 128)] = by_plane[q : q + 1, k * 128 : (k + 1) * 128]

    def decode_block(block, carry):
        size = ROWS // ROW_BLOCKS
        rows = pl.ds(pl.multiple_of(block * size, size), size)
        pltpu.make_async_copy(geno.at[rows], words.at[rows], word_sem.at[block]).wait()
        def decode(i, inner):
            at = pl.ds(pl.multiple_of(block * size + i * 16, 16), 16)
            word = words[at, :]
            for k in range(PLANES):
                codes[k, at, :] = ((word >> (2 * k)) & 3).astype(F32).astype(BF16)
            return inner

        return lax.fori_loop(0, size // 16, decode, carry)

    lax.fori_loop(0, ROW_BLOCKS, decode_block, 0)

    for copy in locals_:
        copy.wait()

    for it in range(ITERS):
        column_sum = jnp.zeros((COLS, FAM), F32)
        for f in range(FAMS):
            column_sum = column_sum + halves[it][f].astype(F32)
        column_sum = jnp.sum(column_sum, axis=1, keepdims=True)

        total[...] = jnp.zeros_like(total)

        def to_markers(k):
            turned = jnp.concatenate([halves[it][f] for f in range(FAMS)], axis=1)
            product = dot(turned, codes[k], 1, 0) - column_sum * twice_freq[k]
            both[k, 0] = product[:, :HALF]
            both[k, 1] = product[:, HALF:]
            core_send[it, k] = both[k, 1 - core].astype(BF16).reshape(CHIPS, BAND, HALF)

        def send_core(k):
            remote(
                core_send.at[it, k],
                core_recv.at[it, k],
                core_sem.at[it, 0, k],
                core_sem.at[it, 1, k],
                partner,
            ).start()

        def over_chips(k):
            arrived(core_recv.at[it, k], core_sem.at[it, 1, k])
            summed = both[k, core].reshape(CHIPS, BAND, HALF) + core_recv[it, k].astype(F32)
            both[k, core] = summed.reshape(COLS, HALF)
            chip_send[it, k] = summed.astype(BF16)
            for slot, to in enumerate(other_chips):
                remote(
                    chip_send.at[it, k, to],
                    chip_recv.at[it, k, slot],
                    chip_sem.at[it, 0, k],
                    chip_sem.at[it, 1, k],
                    {"animal": to * 2 + core},
                ).start()

        def to_chips(k):
            arrived(chip_recv.at[it, k], chip_sem.at[it, 1, k])
            mine = both[k, core, pl.ds(pl.multiple_of(chip * BAND, BAND), BAND), :]
            for d in range(CHIPS - 1):
                mine = mine + chip_recv[it, k, d].astype(F32)
            whole[it, k, core, chip] = mine.astype(BF16)
            for to in other_chips:
                remote(
                    whole.at[it, k, core, chip],
                    whole.at[it, k, core, chip],
                    back_sem.at[it, 0, k],
                    back_sem.at[it, 1, k],
                    {"animal": to * 2 + core},
                ).start()

        def to_core(k):
            arrived(chip_recv.at[it, k], back_sem.at[it, 1, k])
            remote(
                whole.at[it, k, core],
                whole.at[it, k, core],
                join_sem.at[it, 0, k],
                join_sem.at[it, 1, k],
                partner,
            ).start()

        def marker_sums(k):
            arrived(core_recv.at[it, k], join_sem.at[it, 1, k])
            lower = whole[it, k, 0].reshape(COLS, HALF)
            upper = whole[it, k, 1].reshape(COLS, HALF)
            sums = jnp.concatenate([lower, upper], axis=1)
            weighed = sums.astype(F32) * twice_freq[k]
            return sums, jnp.sum(weighed, axis=1, keepdims=True)

        def to_animals(k, shift):
            sums, weighed = marker_sums(k)
            total[...] += dot(codes[k], sums, 1, 1)
            return shift + weighed

        def out_step(t, carry):
            to_markers(t)
            send_core(t)
            over_chips(t - 1)
            return carry

        to_markers(0)
        if it == 0:
                pl.semaphore_wait(barrier, ANIMAL - 1 + SNP - 1)

                for d in range(1, RSPAN + 1):

                    @pl.when(animal >= d)
                    def _():
                        remote(
                            rel_vector,
                            request[d - 1],
                            request_sem.at[0, d - 1],
                            request_sem.at[1, d - 1],
                            {"animal": animal - d},
                        ).start()


        send_core(0)
        lax.fori_loop(1, PLANES, out_step, 0)
        over_chips(PLANES - 1)

        def back_step(k, carry):
            to_chips(k)
            return carry

        lax.fori_loop(0, PLANES, back_step, 0)

        if it == 0:

            for d in range(1, RSPAN + 1):

                @pl.when(animal + d < ANIMAL)
                def _():
                    arrived(request[d - 1], request_sem.at[1, d - 1])
                    copy = pltpu.make_async_copy(
                        request[d - 1], request_scalar[d - 1], local_sem.at[3]
                    )
                    copy.start()
                    copy.wait()

        for d in range(1, RSPAN + 1):

            @pl.when(animal + d < ANIMAL)
            def _():
                for i in range(2):
                    wanted = lax.rem(request_scalar[d - 1][family_first + i], FAMS)
                    rel_send[it, d - 1, i] = halves[it][wanted]
                remote(
                    rel_send.at[it, d - 1],
                    rel_recv[it].at[d - 1],
                    rel_sem.at[it, 0, d - 1],
                    rel_sem.at[it, 1, d - 1],
                    {"animal": animal + d},
                ).start()

        to_core(0)

        def in_step(k, shift):
            to_core(k)
            return to_animals(k - 1, shift)

        shift = lax.fori_loop(1, PLANES, in_step, jnp.zeros((COLS, 1), F32))
        sums, weighed = marker_sums(PLANES - 1)
        shift = jnp.broadcast_to(shift + weighed, (COLS, COLS)).T[:1]

        def last_block(d, carry):
            to = peer(d)
            rows = pl.ds(pl.multiple_of(to * SHARE, SHARE), SHARE)
            block = total[rows, :] - shift + dot(codes[PLANES - 1, rows, :], sums, 1, 1)

            @pl.when(d < SNP - 1)
            def _():
                gen_send[it, d] = block.astype(BF16)
                remote(
                    gen_send.at[it, d],
                    gen_recv.at[it, d],
                    gen_sem.at[it, 0],
                    gen_sem.at[it, 1],
                    {"snp": to},
                ).start()

            @pl.when(d == SNP - 1)
            def _():
                total[rows, :] = block

            return carry

        lax.fori_loop(0, SNP, last_block, 0)

        for d in range(1, RSPAN + 1):

            @pl.when(animal >= d)
            def _():
                arrived(rel_recv[it].at[d - 1], rel_sem.at[it, 1, d - 1])

        pedigree = []
        for i in range(2):
            family = family_first + i
            relative = rel_family[family]
            distance = animal - relative // FAMS
            here = halves[it][lax.rem(relative, FAMS)]
            there = rel_recv[it][jnp.clip(distance - 1, 0, RSPAN - 1), i]
            taken = jnp.where(distance == 0, here.astype(F32), there.astype(F32))
            taken = jnp.where(lane_slot < rel_count[family], taken, 0.0).astype(BF16)
            pedigree.append(
                dot(own_now[i], halves[it][family], 1, 1) + dot(couple_now[i], taken, 1, 1)
            )

        arrived(gen_recv.at[it], gen_sem.at[it, 1])
        for i in range(2):
            own_rows = pl.ds(pl.multiple_of(snp * SHARE + i * FAM, FAM), FAM)
            genomic = total[own_rows, :]
            for d in range(SNP - 1):
                genomic = genomic + gen_recv[it, d, pl.ds(i * FAM, FAM), :].astype(F32)
            residual = live[i] * (
                right_now[pl.ds(i * FAM, FAM), :]
                - share_now[i]
                - GEN_WEIGHT / SNPS * genomic
                - pedigree[i]
            )
            scale = jnp.broadcast_to(step_scale[pl.ds(family_first + i, 1), :], (FAM, FAM)).T
            updated = share_now[i] + scale * residual
            if it + 1 < ITERS:
                share_now[i] = updated
                halves[it + 1][family_first + i] = updated.T.astype(BF16)
            else:
                out[0, pl.ds(i * FAM, FAM), :] = updated
                out[1, pl.ds(i * FAM, FAM), :] = residual

        if it + 1 < ITERS:
            mine = halves[it + 1].at[pl.ds(family_first, 2)]
            for d in range(SNP - 1):
                remote(
                    mine,
                    mine,
                    half_sem.at[0],
                    half_sem.at[1],
                    {"snp": peer(d)},
                ).start()
            arrived(halves[it + 1].at[pl.ds(0, 14)], half_sem.at[1])

    arrived(halves[1].at[pl.ds(0, 14)], half_sem.at[0])
    for d in range(1, RSPAN + 1):

        @pl.when(animal >= d)
        def _():
            arrived(rel_vector, request_sem.at[0, d - 1])

        @pl.when(animal + d < ANIMAL)
        def _():
            for it in range(ITERS):
                arrived(rel_send.at[it, d - 1], rel_sem.at[it, 0, d - 1])

    for it in range(ITERS):
        arrived(gen_send.at[it], gen_sem.at[it, 0])

        def sent(k, carry):
            arrived(core_send.at[it, k], core_sem.at[it, 0, k])
            arrived(core_send.at[it, k], join_sem.at[it, 0, k])
            arrived(chip_recv.at[it, k], chip_sem.at[it, 0, k])
            arrived(chip_recv.at[it, k], back_sem.at[it, 0, k])
            return carry

        lax.fori_loop(0, PLANES, sent, 0)


def per_device(
    genotypes,
    allele_frequency,
    family_size,
    rel_family,
    rel_count,
    own_block,
    rel_block,
    prior_solution,
    right_side,
    step_scale,
):
    vmem = pl.BlockSpec(memory_space=pltpu.VMEM)
    smem = pl.BlockSpec(memory_space=pltpu.SMEM)
    hbm = pl.BlockSpec(memory_space=pl.ANY)
    dma = pltpu.SemaphoreType.DMA
    both = pl.pallas_call(
        kernel,
        out_shape=jax.ShapeDtypeStruct((2, SHARE, COLS), F32),
        in_specs=[hbm, vmem, smem, smem, vmem, smem, hbm, hbm, vmem, hbm, vmem],
        out_specs=vmem,
        scratch_shapes=[
            pltpu.VMEM((ROWS, WORDS), jnp.int32),
            pltpu.VMEM((PLANES, ROWS, WORDS), BF16),
            pltpu.VMEM((FAMS, COLS, FAM), BF16),
            pltpu.VMEM((FAMS, COLS, FAM), BF16),
            pltpu.VMEM((PLANES, 2, COLS, HALF), F32),
            pltpu.VMEM((ITERS, PLANES, CHIPS, BAND, HALF), BF16),
            pltpu.VMEM((ITERS, PLANES, CHIPS, BAND, HALF), BF16),
            pltpu.VMEM((ITERS, PLANES, CHIPS, BAND, HALF), BF16),
            pltpu.VMEM((ITERS, PLANES, CHIPS - 1, BAND, HALF), BF16),
            pltpu.VMEM((ITERS, PLANES, 2, CHIPS, BAND, HALF), BF16),
            pltpu.VMEM((ROWS, COLS), F32),
            pltpu.VMEM((ITERS, SNP - 1, SHARE, COLS), BF16),
            pltpu.VMEM((ITERS, SNP - 1, SHARE, COLS), BF16),
            pltpu.VMEM((2, FAM, COLS), F32),
            pltpu.VMEM((2, FAM, FAM), BF16),
            pltpu.VMEM((2, FAM, FAM), BF16),
            pltpu.VMEM((SHARE, COLS), F32),
            pltpu.VMEM((ITERS, RSPAN, 2, COLS, FAM), BF16),
            pltpu.VMEM((RSPAN, 2, COLS, FAM), BF16),
            pltpu.VMEM((RSPAN, 2, COLS, FAM), BF16),
            *[pltpu.VMEM((FAMS,), jnp.int32)] * RSPAN,
            *[pltpu.SMEM((FAMS,), jnp.int32)] * RSPAN,
            pltpu.VMEM((PLANES, 1, WORDS), F32),
            dma((ROW_BLOCKS,)),
            dma((4,)),
            dma((2, RSPAN)),
            dma((ITERS, 2, PLANES)),
            dma((ITERS, 2, PLANES)),
            dma((ITERS, 2, PLANES)),
            dma((ITERS, 2, PLANES)),
            dma((ITERS, 2)),
            dma((2,)),
            dma((ITERS, 2, RSPAN)),
        ],
        compiler_params=pltpu.CompilerParams(
            collective_id=0, has_side_effects=True, vmem_limit_bytes=66 * 10**6
        ),
        name="blup",
    )(
        genotypes,
        allele_frequency.reshape(PLANES * WORDS // 128, 128),
        family_size,
        rel_family,
        rel_family,
        rel_count,
        own_block,
        rel_block,
        prior_solution,
        right_side,
        step_scale.reshape(FAMS, FAM),
    )
    return both[0], both[1]


def solution(mesh):
    in_specs = (
        P("animal", "snp"),
        P("snp"),
        P("animal"),
        P("animal"),
        P("animal"),
        P("animal", None, None),
        P("animal", None, None),
        P("animal", None),
        P("animal", None),
        P("animal"),
    )
    out_specs = (P(("animal", "snp"), None), P(("animal", "snp"), None))
    return jax.shard_map(
        per_device, mesh=mesh, in_specs=in_specs, out_specs=out_specs, check_vma=False
    )
```

```python
import jax
import jax.numpy as jnp
from jax import lax
from jax.experimental import pallas as pl
from jax.experimental.pallas import tpu as pltpu
from jax.sharding import PartitionSpec as P

SNPS = 49152
ITERS = 2
RSPAN = 3
GEN_WEIGHT = 6.0
PLANES = 6
EARLY = 3
FAM = 128
COLS = 128
ANIMAL = 16
SNP = 8
CHIPS = 8
ROWS = 2048
WORDS = 1024
FAMS = 16
SHARE = 256
HALF = 512
BAND = 16
ROW_BLOCKS = 8

F32 = jnp.float32
BF16 = jnp.bfloat16
F8 = jnp.float8_e4m3fn


def dot(a, b, ca, cb):
    return lax.dot_general(a, b, (((ca,), (cb,)), ((), ())), preferred_element_type=F32)


def remote(src, dst, send, recv, where):
    return pltpu.make_async_remote_copy(
        src_ref=src,
        dst_ref=dst,
        send_sem=send,
        recv_sem=recv,
        device_id=where,
        device_id_type=pl.DeviceIdType.MESH,
    )


def arrived(ref, sem):
    pltpu.make_async_copy(ref, ref, sem).wait()


def kernel(
    geno,
    freq,
    family_size,
    rel_family,
    rel_vector,
    rel_count,
    own_block,
    rel_block,
    prior,
    right_side,
    step_scale,
    out,
    words,
    codes,
    half_first,
    half_second,
    both,
    core_send,
    core_recv,
    chip_send,
    chip_recv,
    whole,
    total,
    gen_send,
    gen_recv,
    share_now,
    own_now,
    couple_now,
    right_now,
    rel_send,
    rel_first,
    rel_second,
    request_one,
    request_two,
    request_three,
    scalar_one,
    scalar_two,
    scalar_three,
    twice_freq,
    word_sem,
    local_sem,
    request_sem,
    core_sem,
    chip_sem,
    back_sem,
    join_sem,
    gen_sem,
    half_sem,
    rel_sem,
):
    animal = lax.axis_index("animal")
    snp = lax.axis_index("snp")
    core = lax.rem(animal, 2)
    chip = animal // 2
    request = (request_one, request_two, request_three)
    request_scalar = (scalar_one, scalar_two, scalar_three)
    partner = {"animal": animal + 1 - 2 * core}
    other_chips = [
        lax.rem(chip // 2 + dz, 4) * 2 + lax.rem(lax.rem(chip, 2) + dx, 2)
        for dz, dx in ((2, 1), (1, 1), (3, 1), (2, 0), (1, 0), (3, 0), (0, 1))
    ]

    def peer(step):
        far = 1 - step // 4
        return lax.rem(snp // 4 + far, 2) * 4 + lax.rem(lax.rem(snp, 4) + 3 - lax.rem(step, 4), 4)


    for block in range(ROW_BLOCKS):
        rows = pl.ds(block * (ROWS // ROW_BLOCKS), ROWS // ROW_BLOCKS)
        pltpu.make_async_copy(geno.at[rows], words.at[rows], word_sem.at[block]).start()
    family_first = snp * 2
    locals_ = [
        pltpu.make_async_copy(own_block.at[pl.ds(family_first, 2)], own_now, local_sem.at[0]),
        pltpu.make_async_copy(rel_block.at[pl.ds(family_first, 2)], couple_now, local_sem.at[1]),
        pltpu.make_async_copy(right_side.at[pl.ds(snp * SHARE, SHARE)], right_now, local_sem.at[2]),
    ]
    for copy in locals_:
        copy.start()
    halves = (half_first, half_second)
    rel_recv = (rel_first, rel_second)
    for ref in rel_recv:
        ref[...] = jnp.zeros_like(ref)

    barrier = pltpu.get_barrier_semaphore()
    for step in range(1, ANIMAL):
        pl.semaphore_signal(
            barrier,
            inc=1,
            device_id={"animal": lax.rem(animal + step, ANIMAL)},
            device_id_type=pl.DeviceIdType.MESH,
        )
    for step in range(1, SNP):
        pl.semaphore_signal(
            barrier,
            inc=1,
            device_id={"snp": lax.rem(snp + step, SNP)},
            device_id_type=pl.DeviceIdType.MESH,
        )

    lane_slot = lax.broadcasted_iota(jnp.int32, (COLS, FAM), 1)
    row_slot = lax.broadcasted_iota(jnp.int32, (FAM, COLS), 0)

    def first_half(f, carry):
        block = prior[pl.ds(pl.multiple_of(f * FAM, FAM), FAM), :]
        turned = block.astype(F32).T
        halves[0][f] = jnp.where(lane_slot < family_size[f], turned, 0.0).astype(BF16)
        return carry

    lax.fori_loop(0, FAMS, first_half, 0)
    live = [
        jnp.where(row_slot < family_size[family_first + i], 1.0, 0.0).astype(F32) for i in range(2)
    ]
    for i in range(2):
        block = prior[pl.ds(pl.multiple_of((family_first + i) * FAM, FAM), FAM), :]
        share_now[i] = live[i] * block.astype(F32)

    lane = lax.broadcasted_iota(jnp.int32, (128, PLANES * 128), 0)
    column = lax.broadcasted_iota(jnp.int32, (128, PLANES * 128), 1)
    marker = PLANES * (column & 127) + (column >> 7)
    by_plane = jnp.zeros((24, PLANES * 128), F32)
    for r in range(PLANES):
        rest = 2.0 * freq[pl.ds(r, 8, stride=PLANES), :]
        parts = []
        for _ in range(3):
            part = rest.astype(BF16).astype(F32)
            parts.append(part)
            rest = rest - part
        chosen = jnp.where(marker == lane + 128 * r, 1.0, 0.0).astype(BF16)
        by_plane = by_plane + dot(jnp.concatenate(parts, axis=0).astype(BF16), chosen, 1, 0)
    by_plane = by_plane[:8] + by_plane[8:16] + by_plane[16:]
    for k in range(PLANES):
        for q in range(8):
            twice_freq[k, :, pl.ds(q * 128, 128)] = by_plane[q : q + 1, k * 128 : (k + 1) * 128]

    def decode_block(block, carry):
        size = ROWS // ROW_BLOCKS
        rows = pl.ds(pl.multiple_of(block * size, size), size)
        pltpu.make_async_copy(geno.at[rows], words.at[rows], word_sem.at[block]).wait()
        def decode(i, inner):
            at = pl.ds(pl.multiple_of(block * size + i * 32, 32), 32)
            word = words[at, :]
            for k in range(EARLY):
                codes[k, at, :] = ((word >> (2 * k)) & 3).astype(F32).astype(F8)
            return inner

        return lax.fori_loop(0, size // 32, decode, carry)

    lax.fori_loop(0, ROW_BLOCKS, decode_block, 0)

    for copy in locals_:
        copy.wait()

    def decode_plane(k):
        def decode(i, carry):
            at = pl.ds(pl.multiple_of(i * 128, 128), 128)
            codes[k, at, :] = ((words[at, :] >> (2 * k)) & 3).astype(F32).astype(F8)
            return carry

        lax.fori_loop(0, ROWS // 128, decode, 0)

    for it in range(ITERS):
        column_sum = jnp.zeros((COLS, FAM), F32)
        for f in range(FAMS):
            column_sum = column_sum + halves[it][f].astype(F32)
        column_sum = jnp.sum(column_sum, axis=1, keepdims=True)

        total[...] = jnp.zeros_like(total)

        def to_markers(k):
            turned = jnp.concatenate([halves[it][f] for f in range(FAMS)], axis=1)
            product = dot(turned, codes[k], 1, 0) - column_sum * twice_freq[k]
            both[k, 0] = product[:, :HALF]
            both[k, 1] = product[:, HALF:]
            core_send[it, k] = both[k, 1 - core].astype(BF16).reshape(CHIPS, BAND, HALF)

        def send_core(k):
            remote(
                core_send.at[it, k],
                core_recv.at[it, k],
                core_sem.at[it, 0, k],
                core_sem.at[it, 1, k],
                partner,
            ).start()

        def over_chips(k):
            arrived(core_recv.at[it, k], core_sem.at[it, 1, k])
            summed = both[k, core].reshape(CHIPS, BAND, HALF) + core_recv[it, k].astype(F32)
            both[k, core] = summed.reshape(COLS, HALF)
            chip_send[it, k] = summed.astype(BF16)
            for slot, to in enumerate(other_chips):
                remote(
                    chip_send.at[it, k, to],
                    chip_recv.at[it, k, slot],
                    chip_sem.at[it, 0, k],
                    chip_sem.at[it, 1, k],
                    {"animal": to * 2 + core},
                ).start()

        def to_chips(k):
            arrived(chip_recv.at[it, k], chip_sem.at[it, 1, k])
            mine = both[k, core, pl.ds(pl.multiple_of(chip * BAND, BAND), BAND), :]
            for d in range(CHIPS - 1):
                mine = mine + chip_recv[it, k, d].astype(F32)
            whole[it, k, core, chip] = mine.astype(BF16)
            for to in other_chips:
                remote(
                    whole.at[it, k, core, chip],
                    whole.at[it, k, core, chip],
                    back_sem.at[it, 0, k],
                    back_sem.at[it, 1, k],
                    {"animal": to * 2 + core},
                ).start()

        def to_core(k):
            arrived(chip_recv.at[it, k], back_sem.at[it, 1, k])
            remote(
                whole.at[it, k, core],
                whole.at[it, k, core],
                join_sem.at[it, 0, k],
                join_sem.at[it, 1, k],
                partner,
            ).start()

        def marker_sums(k):
            arrived(core_recv.at[it, k], join_sem.at[it, 1, k])
            lower = whole[it, k, 0].reshape(COLS, HALF)
            upper = whole[it, k, 1].reshape(COLS, HALF)
            sums = jnp.concatenate([lower, upper], axis=1)
            sums = sums.astype(F32)
            weighed = jnp.sum(sums * twice_freq[k], axis=1, keepdims=True)
            largest = jnp.max(jnp.max(jnp.abs(sums), axis=1, keepdims=True), axis=0, keepdims=True)
            unit = jnp.maximum(largest, 1e-30) * (1 / 224)
            scaled = sums * (1 / unit)
            high = scaled.astype(F8)
            low = ((scaled - high.astype(F32)) * 16).astype(F8)
            return jnp.concatenate([high, low], axis=0), unit, weighed

        def animal_product(rows_codes, sums, unit):
            pair = dot(rows_codes, sums, 1, 1)
            return (pair[:, :COLS] + pair[:, COLS:] * (1 / 16)) * unit

        def to_animals(k, shift):
            sums, unit, weighed = marker_sums(k)
            total[...] += animal_product(codes[k], sums, unit)
            return shift + weighed

        def out_step(t, carry):
            if it == 0:

                @pl.when(t >= EARLY)
                def _():
                    decode_plane(t)

            to_markers(t)
            send_core(t)
            over_chips(t - 1)
            return carry

        to_markers(0)
        if it == 0:
                pl.semaphore_wait(barrier, ANIMAL - 1 + SNP - 1)

                for d in range(1, RSPAN + 1):

                    @pl.when(animal >= d)
                    def _():
                        remote(
                            rel_vector,
                            request[d - 1],
                            request_sem.at[0, d - 1],
                            request_sem.at[1, d - 1],
                            {"animal": animal - d},
                        ).start()


        send_core(0)
        lax.fori_loop(1, PLANES, out_step, 0)
        over_chips(PLANES - 1)

        def back_step(k, carry):
            to_chips(k)
            return carry

        lax.fori_loop(0, PLANES, back_step, 0)

        if it == 0:

            for d in range(1, RSPAN + 1):

                @pl.when(animal + d < ANIMAL)
                def _():
                    arrived(request[d - 1], request_sem.at[1, d - 1])
                    copy = pltpu.make_async_copy(
                        request[d - 1], request_scalar[d - 1], local_sem.at[3]
                    )
                    copy.start()
                    copy.wait()

        for d in range(1, RSPAN + 1):

            @pl.when(animal + d < ANIMAL)
            def _():
                for i in range(2):
                    wanted = lax.rem(request_scalar[d - 1][family_first + i], FAMS)
                    rel_send[it, d - 1, i] = halves[it][wanted]
                remote(
                    rel_send.at[it, d - 1],
                    rel_recv[it].at[d - 1],
                    rel_sem.at[it, 0, d - 1],
                    rel_sem.at[it, 1, d - 1],
                    {"animal": animal + d},
                ).start()

        to_core(0)

        def in_step(k, shift):
            to_core(k)
            return to_animals(k - 1, shift)

        shift = lax.fori_loop(1, PLANES, in_step, jnp.zeros((COLS, 1), F32))
        sums, unit, weighed = marker_sums(PLANES - 1)
        shift = jnp.broadcast_to(shift + weighed, (COLS, COLS)).T[:1]

        def last_block(d, carry):
            to = peer(d)
            rows = pl.ds(pl.multiple_of(to * SHARE, SHARE), SHARE)
            part = animal_product(codes[PLANES - 1, rows, :], sums, unit)
            block = total[rows, :] - shift + part

            @pl.when(d < SNP - 1)
            def _():
                gen_send[it, d] = block.astype(BF16)
                remote(
                    gen_send.at[it, d],
                    gen_recv.at[it, d],
                    gen_sem.at[it, 0],
                    gen_sem.at[it, 1],
                    {"snp": to},
                ).start()

            @pl.when(d == SNP - 1)
            def _():
                total[rows, :] = block

            return carry

        lax.fori_loop(0, SNP, last_block, 0)

        for d in range(1, RSPAN + 1):

            @pl.when(animal >= d)
            def _():
                arrived(rel_recv[it].at[d - 1], rel_sem.at[it, 1, d - 1])

        pedigree = []
        for i in range(2):
            family = family_first + i
            relative = rel_family[family]
            distance = animal - relative // FAMS
            here = halves[it][lax.rem(relative, FAMS)]
            there = rel_recv[it][jnp.clip(distance - 1, 0, RSPAN - 1), i]
            taken = jnp.where(distance == 0, here.astype(F32), there.astype(F32))
            taken = jnp.where(lane_slot < rel_count[family], taken, 0.0).astype(BF16)
            pedigree.append(
                dot(own_now[i], halves[it][family], 1, 1) + dot(couple_now[i], taken, 1, 1)
            )

        arrived(gen_recv.at[it], gen_sem.at[it, 1])
        for i in range(2):
            own_rows = pl.ds(pl.multiple_of(snp * SHARE + i * FAM, FAM), FAM)
            genomic = total[own_rows, :]
            for d in range(SNP - 1):
                genomic = genomic + gen_recv[it, d, pl.ds(i * FAM, FAM), :].astype(F32)
            residual = live[i] * (
                right_now[pl.ds(i * FAM, FAM), :]
                - share_now[i]
                - GEN_WEIGHT / SNPS * genomic
                - pedigree[i]
            )
            scale = jnp.broadcast_to(step_scale[pl.ds(family_first + i, 1), :], (FAM, FAM)).T
            updated = share_now[i] + scale * residual
            if it + 1 < ITERS:
                share_now[i] = updated
                halves[it + 1][family_first + i] = updated.T.astype(BF16)
            else:
                out[0, pl.ds(i * FAM, FAM), :] = updated
                out[1, pl.ds(i * FAM, FAM), :] = residual

        if it + 1 < ITERS:
            mine = halves[it + 1].at[pl.ds(family_first, 2)]
            for d in range(SNP - 1):
                remote(
                    mine,
                    mine,
                    half_sem.at[0],
                    half_sem.at[1],
                    {"snp": peer(d)},
                ).start()
            arrived(halves[it + 1].at[pl.ds(0, 14)], half_sem.at[1])

    arrived(halves[1].at[pl.ds(0, 14)], half_sem.at[0])
    for d in range(1, RSPAN + 1):

        @pl.when(animal >= d)
        def _():
            arrived(rel_vector, request_sem.at[0, d - 1])

        @pl.when(animal + d < ANIMAL)
        def _():
            for it in range(ITERS):
                arrived(rel_send.at[it, d - 1], rel_sem.at[it, 0, d - 1])

    for it in range(ITERS):
        arrived(gen_send.at[it], gen_sem.at[it, 0])

        def sent(k, carry):
            arrived(core_send.at[it, k], core_sem.at[it, 0, k])
            arrived(core_send.at[it, k], join_sem.at[it, 0, k])
            arrived(chip_recv.at[it, k], chip_sem.at[it, 0, k])
            arrived(chip_recv.at[it, k], back_sem.at[it, 0, k])
            return carry

        lax.fori_loop(0, PLANES, sent, 0)


def per_device(
    genotypes,
    allele_frequency,
    family_size,
    rel_family,
    rel_count,
    own_block,
    rel_block,
    prior_solution,
    right_side,
    step_scale,
):
    vmem = pl.BlockSpec(memory_space=pltpu.VMEM)
    smem = pl.BlockSpec(memory_space=pltpu.SMEM)
    hbm = pl.BlockSpec(memory_space=pl.ANY)
    dma = pltpu.SemaphoreType.DMA
    both = pl.pallas_call(
        kernel,
        out_shape=jax.ShapeDtypeStruct((2, SHARE, COLS), F32),
        in_specs=[hbm, vmem, smem, smem, vmem, smem, hbm, hbm, vmem, hbm, vmem],
        out_specs=vmem,
        scratch_shapes=[
            pltpu.VMEM((ROWS, WORDS), jnp.int32),
            pltpu.VMEM((PLANES, ROWS, WORDS), F8),
            pltpu.VMEM((FAMS, COLS, FAM), BF16),
            pltpu.VMEM((FAMS, COLS, FAM), BF16),
            pltpu.VMEM((PLANES, 2, COLS, HALF), F32),
            pltpu.VMEM((ITERS, PLANES, CHIPS, BAND, HALF), BF16),
            pltpu.VMEM((ITERS, PLANES, CHIPS, BAND, HALF), BF16),
            pltpu.VMEM((ITERS, PLANES, CHIPS, BAND, HALF), BF16),
            pltpu.VMEM((ITERS, PLANES, CHIPS - 1, BAND, HALF), BF16),
            pltpu.VMEM((ITERS, PLANES, 2, CHIPS, BAND, HALF), BF16),
            pltpu.VMEM((ROWS, COLS), F32),
            pltpu.VMEM((ITERS, SNP - 1, SHARE, COLS), BF16),
            pltpu.VMEM((ITERS, SNP - 1, SHARE, COLS), BF16),
            pltpu.VMEM((2, FAM, COLS), F32),
            pltpu.VMEM((2, FAM, FAM), BF16),
            pltpu.VMEM((2, FAM, FAM), BF16),
            pltpu.VMEM((SHARE, COLS), F32),
            pltpu.VMEM((ITERS, RSPAN, 2, COLS, FAM), BF16),
            pltpu.VMEM((RSPAN, 2, COLS, FAM), BF16),
            pltpu.VMEM((RSPAN, 2, COLS, FAM), BF16),
            *[pltpu.VMEM((FAMS,), jnp.int32)] * RSPAN,
            *[pltpu.SMEM((FAMS,), jnp.int32)] * RSPAN,
            pltpu.VMEM((PLANES, 1, WORDS), F32),
            dma((ROW_BLOCKS,)),
            dma((4,)),
            dma((2, RSPAN)),
            dma((ITERS, 2, PLANES)),
            dma((ITERS, 2, PLANES)),
            dma((ITERS, 2, PLANES)),
            dma((ITERS, 2, PLANES)),
            dma((ITERS, 2)),
            dma((2,)),
            dma((ITERS, 2, RSPAN)),
        ],
        compiler_params=pltpu.CompilerParams(
            collective_id=0, has_side_effects=True, vmem_limit_bytes=66 * 10**6
        ),
        name="blup",
    )(
        genotypes,
        allele_frequency.reshape(PLANES * WORDS // 128, 128),
        family_size,
        rel_family,
        rel_family,
        rel_count,
        own_block,
        rel_block,
        prior_solution,
        right_side,
        step_scale.reshape(FAMS, FAM),
    )
    return both[0], both[1]


def solution(mesh):
    in_specs = (
        P("animal", "snp"),
        P("snp"),
        P("animal"),
        P("animal"),
        P("animal"),
        P("animal", None, None),
        P("animal", None, None),
        P("animal", None),
        P("animal", None),
        P("animal"),
    )
    out_specs = (P(("animal", "snp"), None), P(("animal", "snp"), None))
    return jax.shard_map(
        per_device, mesh=mesh, in_specs=in_specs, out_specs=out_specs, check_vma=False
    )
```

```python
import jax
import jax.numpy as jnp
from jax import lax
from jax.experimental import pallas as pl
from jax.experimental.pallas import tpu as pltpu
from jax.sharding import PartitionSpec as P

SNPS = 49152
ITERS = 2
RSPAN = 3
GEN_WEIGHT = 6.0
PLANES = 6
EARLY = 3
FAM = 128
COLS = 128
ANIMAL = 16
SNP = 8
CHIPS = 8
ROWS = 2048
WORDS = 1024
FAMS = 16
SHARE = 256
HALF = 512
BAND = 16
ROW_BLOCKS = 8

F32 = jnp.float32
BF16 = jnp.bfloat16
F8 = jnp.float8_e4m3fn


def dot(a, b, ca, cb):
    return lax.dot_general(a, b, (((ca,), (cb,)), ((), ())), preferred_element_type=F32)


def remote(src, dst, send, recv, where):
    return pltpu.make_async_remote_copy(
        src_ref=src,
        dst_ref=dst,
        send_sem=send,
        recv_sem=recv,
        device_id=where,
        device_id_type=pl.DeviceIdType.MESH,
    )


def arrived(ref, sem):
    pltpu.make_async_copy(ref, ref, sem).wait()


def kernel(
    geno,
    freq,
    family_size,
    rel_family,
    rel_vector,
    rel_count,
    own_block,
    rel_block,
    prior,
    right_side,
    step_scale,
    out,
    words,
    codes,
    half_first,
    half_second,
    both,
    core_send,
    core_recv,
    chip_send,
    chip_recv,
    whole,
    total,
    gen_send,
    gen_recv,
    share_now,
    own_now,
    couple_now,
    right_now,
    rel_send,
    rel_first,
    rel_second,
    request_one,
    request_two,
    request_three,
    scalar_one,
    scalar_two,
    scalar_three,
    twice_freq,
    word_sem,
    local_sem,
    request_sem,
    core_sem,
    chip_sem,
    back_sem,
    join_sem,
    gen_sem,
    half_sem,
    rel_sem,
):
    animal = lax.axis_index("animal")
    snp = lax.axis_index("snp")
    core = lax.rem(animal, 2)
    chip = animal // 2
    request = (request_one, request_two, request_three)
    request_scalar = (scalar_one, scalar_two, scalar_three)
    partner = {"animal": animal + 1 - 2 * core}
    other_chips = [
        lax.rem(chip // 2 + dz, 4) * 2 + lax.rem(lax.rem(chip, 2) + dx, 2)
        for dz, dx in ((2, 1), (1, 1), (3, 1), (2, 0), (1, 0), (3, 0), (0, 1))
    ]

    def peer(step):
        far = 1 - step // 4
        return lax.rem(snp // 4 + far, 2) * 4 + lax.rem(lax.rem(snp, 4) + 3 - lax.rem(step, 4), 4)


    for block in range(ROW_BLOCKS):
        rows = pl.ds(block * (ROWS // ROW_BLOCKS), ROWS // ROW_BLOCKS)
        pltpu.make_async_copy(geno.at[rows], words.at[rows], word_sem.at[block]).start()
    family_first = snp * 2
    locals_ = [
        pltpu.make_async_copy(own_block.at[pl.ds(family_first, 2)], own_now, local_sem.at[0]),
        pltpu.make_async_copy(rel_block.at[pl.ds(family_first, 2)], couple_now, local_sem.at[1]),
        pltpu.make_async_copy(right_side.at[pl.ds(snp * SHARE, SHARE)], right_now, local_sem.at[2]),
    ]
    for copy in locals_:
        copy.start()
    halves = (half_first, half_second)
    rel_recv = (rel_first, rel_second)
    for ref in rel_recv:
        ref[...] = jnp.zeros_like(ref)

    barrier = pltpu.get_barrier_semaphore()
    for step in range(1, ANIMAL):
        pl.semaphore_signal(
            barrier,
            inc=1,
            device_id={"animal": lax.rem(animal + step, ANIMAL)},
            device_id_type=pl.DeviceIdType.MESH,
        )
    for step in range(1, SNP):
        pl.semaphore_signal(
            barrier,
            inc=1,
            device_id={"snp": lax.rem(snp + step, SNP)},
            device_id_type=pl.DeviceIdType.MESH,
        )

    lane_slot = lax.broadcasted_iota(jnp.int32, (COLS, FAM), 1)
    row_slot = lax.broadcasted_iota(jnp.int32, (FAM, COLS), 0)

    def first_half(f, carry):
        block = prior[pl.ds(pl.multiple_of(f * FAM, FAM), FAM), :]
        turned = block.astype(F32).T
        halves[0][f] = jnp.where(lane_slot < family_size[f], turned, 0.0).astype(BF16)
        return carry

    lax.fori_loop(0, FAMS, first_half, 0)
    live = [
        jnp.where(row_slot < family_size[family_first + i], 1.0, 0.0).astype(F32) for i in range(2)
    ]
    for i in range(2):
        block = prior[pl.ds(pl.multiple_of((family_first + i) * FAM, FAM), FAM), :]
        share_now[i] = live[i] * block.astype(F32)

    lane = lax.broadcasted_iota(jnp.int32, (128, PLANES * 128), 0)
    column = lax.broadcasted_iota(jnp.int32, (128, PLANES * 128), 1)
    marker = PLANES * (column & 127) + (column >> 7)
    by_plane = jnp.zeros((24, PLANES * 128), F32)
    for r in range(PLANES):
        rest = 2.0 * freq[pl.ds(r, 8, stride=PLANES), :]
        parts = []
        for _ in range(3):
            part = rest.astype(BF16).astype(F32)
            parts.append(part)
            rest = rest - part
        chosen = jnp.where(marker == lane + 128 * r, 1.0, 0.0).astype(BF16)
        by_plane = by_plane + dot(jnp.concatenate(parts, axis=0).astype(BF16), chosen, 1, 0)
    by_plane = by_plane[:8] + by_plane[8:16] + by_plane[16:]
    for k in range(PLANES):
        for q in range(8):
            twice_freq[k, :, pl.ds(q * 128, 128)] = by_plane[q : q + 1, k * 128 : (k + 1) * 128]

    def decode_block(block, carry):
        size = ROWS // ROW_BLOCKS
        rows = pl.ds(pl.multiple_of(block * size, size), size)
        pltpu.make_async_copy(geno.at[rows], words.at[rows], word_sem.at[block]).wait()
        def decode(i, inner):
            at = pl.ds(pl.multiple_of(block * size + i * 32, 32), 32)
            word = words[at, :]
            for k in range(EARLY):
                codes[k, at, :] = ((word >> (2 * k)) & 3).astype(F32).astype(F8)
            return inner

        return lax.fori_loop(0, size // 32, decode, carry)

    lax.fori_loop(0, ROW_BLOCKS, decode_block, 0)

    for copy in locals_:
        copy.wait()

    def decode_plane(k):
        def decode(i, carry):
            at = pl.ds(pl.multiple_of(i * 128, 128), 128)
            codes[k, at, :] = ((words[at, :] >> (2 * k)) & 3).astype(F32).astype(F8)
            return carry

        lax.fori_loop(0, ROWS // 128, decode, 0)

    for it in range(ITERS):
        column_sum = jnp.zeros((COLS, FAM), F32)
        for f in range(FAMS):
            column_sum = column_sum + halves[it][f].astype(F32)
        column_sum = jnp.sum(column_sum, axis=1, keepdims=True)

        total[...] = jnp.zeros_like(total)

        def to_markers(k):
            turned = jnp.concatenate([halves[it][f] for f in range(FAMS)], axis=1)
            product = dot(turned, codes[k], 1, 0) - column_sum * twice_freq[k]
            both[k, 0] = product[:, :HALF]
            both[k, 1] = product[:, HALF:]
            core_send[it, k] = both[k, 1 - core].astype(BF16).reshape(CHIPS, BAND, HALF)

        def send_core(k):
            remote(
                core_send.at[it, k],
                core_recv.at[it, k],
                core_sem.at[it, 0, k],
                core_sem.at[it, 1, k],
                partner,
            ).start()

        def over_chips(k):
            arrived(core_recv.at[it, k], core_sem.at[it, 1, k])
            summed = both[k, core].reshape(CHIPS, BAND, HALF) + core_recv[it, k].astype(F32)
            both[k, core] = summed.reshape(COLS, HALF)
            chip_send[it, k] = summed.astype(BF16)
            for slot, to in enumerate(other_chips):
                remote(
                    chip_send.at[it, k, to],
                    chip_recv.at[it, k, slot],
                    chip_sem.at[it, 0, k],
                    chip_sem.at[it, 1, k],
                    {"animal": to * 2 + core},
                ).start()

        def to_chips(k):
            arrived(chip_recv.at[it, k], chip_sem.at[it, 1, k])
            mine = both[k, core, pl.ds(pl.multiple_of(chip * BAND, BAND), BAND), :]
            for d in range(CHIPS - 1):
                mine = mine + chip_recv[it, k, d].astype(F32)
            whole[it, k, core, chip] = mine.astype(BF16)
            for to in other_chips:
                remote(
                    whole.at[it, k, core, chip],
                    whole.at[it, k, core, chip],
                    back_sem.at[it, 0, k],
                    back_sem.at[it, 1, k],
                    {"animal": to * 2 + core},
                ).start()

        def to_core(k):
            arrived(chip_recv.at[it, k], back_sem.at[it, 1, k])
            remote(
                whole.at[it, k, core],
                whole.at[it, k, core],
                join_sem.at[it, 0, k],
                join_sem.at[it, 1, k],
                partner,
            ).start()

        def marker_sums(k):
            arrived(core_recv.at[it, k], join_sem.at[it, 1, k])
            lower = whole[it, k, 0].reshape(COLS, HALF)
            upper = whole[it, k, 1].reshape(COLS, HALF)
            sums = jnp.concatenate([lower, upper], axis=1)
            sums = sums.astype(F32)
            largest = jnp.max(jnp.max(jnp.abs(sums), axis=1, keepdims=True), axis=0, keepdims=True)
            unit = jnp.maximum(largest, 1e-30) * (1 / 224)
            scaled = sums * (1 / unit)
            high = scaled.astype(F8)
            low = ((scaled - high.astype(F32)) * 16).astype(F8)
            kept = high.astype(F32) + low.astype(F32) * (1 / 16)
            weighed = jnp.sum(kept * twice_freq[k], axis=1, keepdims=True) * unit
            return jnp.concatenate([high, low], axis=0), unit, weighed

        def animal_product(rows_codes, sums, unit):
            pair = dot(rows_codes, sums, 1, 1)
            return (pair[:, :COLS] + pair[:, COLS:] * (1 / 16)) * unit

        def to_animals(k, shift):
            sums, unit, weighed = marker_sums(k)
            total[...] += animal_product(codes[k], sums, unit)
            return shift + weighed

        def out_step(t, carry):
            if it == 0:

                @pl.when(t >= EARLY)
                def _():
                    decode_plane(t)

            to_markers(t)
            send_core(t)
            over_chips(t - 1)
            return carry

        to_markers(0)
        if it == 0:
                pl.semaphore_wait(barrier, ANIMAL - 1 + SNP - 1)

                for d in range(1, RSPAN + 1):

                    @pl.when(animal >= d)
                    def _():
                        remote(
                            rel_vector,
                            request[d - 1],
                            request_sem.at[0, d - 1],
                            request_sem.at[1, d - 1],
                            {"animal": animal - d},
                        ).start()


        send_core(0)
        lax.fori_loop(1, PLANES, out_step, 0)
        over_chips(PLANES - 1)

        def back_step(k, carry):
            to_chips(k)
            return carry

        lax.fori_loop(0, PLANES, back_step, 0)

        if it == 0:

            for d in range(1, RSPAN + 1):

                @pl.when(animal + d < ANIMAL)
                def _():
                    arrived(request[d - 1], request_sem.at[1, d - 1])
                    copy = pltpu.make_async_copy(
                        request[d - 1], request_scalar[d - 1], local_sem.at[3]
                    )
                    copy.start()
                    copy.wait()

        for d in range(1, RSPAN + 1):

            @pl.when(animal + d < ANIMAL)
            def _():
                for i in range(2):
                    wanted = lax.rem(request_scalar[d - 1][family_first + i], FAMS)
                    rel_send[it, d - 1, i] = halves[it][wanted]
                remote(
                    rel_send.at[it, d - 1],
                    rel_recv[it].at[d - 1],
                    rel_sem.at[it, 0, d - 1],
                    rel_sem.at[it, 1, d - 1],
                    {"animal": animal + d},
                ).start()

        to_core(0)

        def in_step(k, shift):
            to_core(k)
            return to_animals(k - 1, shift)

        shift = lax.fori_loop(1, PLANES, in_step, jnp.zeros((COLS, 1), F32))
        sums, unit, weighed = marker_sums(PLANES - 1)
        shift = jnp.broadcast_to(shift + weighed, (COLS, COLS)).T[:1]

        def last_block(d, carry):
            to = peer(d)
            rows = pl.ds(pl.multiple_of(to * SHARE, SHARE), SHARE)
            part = animal_product(codes[PLANES - 1, rows, :], sums, unit)
            block = total[rows, :] - shift + part

            @pl.when(d < SNP - 1)
            def _():
                gen_send[it, d] = block.astype(BF16)
                remote(
                    gen_send.at[it, d],
                    gen_recv.at[it, d],
                    gen_sem.at[it, 0],
                    gen_sem.at[it, 1],
                    {"snp": to},
                ).start()

            @pl.when(d == SNP - 1)
            def _():
                total[rows, :] = block

            return carry

        lax.fori_loop(0, SNP, last_block, 0)

        for d in range(1, RSPAN + 1):

            @pl.when(animal >= d)
            def _():
                arrived(rel_recv[it].at[d - 1], rel_sem.at[it, 1, d - 1])

        pedigree = []
        for i in range(2):
            family = family_first + i
            relative = rel_family[family]
            distance = animal - relative // FAMS
            here = halves[it][lax.rem(relative, FAMS)]
            there = rel_recv[it][jnp.clip(distance - 1, 0, RSPAN - 1), i]
            taken = jnp.where(distance == 0, here.astype(F32), there.astype(F32))
            taken = jnp.where(lane_slot < rel_count[family], taken, 0.0).astype(BF16)
            pedigree.append(
                dot(own_now[i], halves[it][family], 1, 1) + dot(couple_now[i], taken, 1, 1)
            )

        arrived(gen_recv.at[it], gen_sem.at[it, 1])
        for i in range(2):
            own_rows = pl.ds(pl.multiple_of(snp * SHARE + i * FAM, FAM), FAM)
            genomic = total[own_rows, :]
            for d in range(SNP - 1):
                genomic = genomic + gen_recv[it, d, pl.ds(i * FAM, FAM), :].astype(F32)
            residual = live[i] * (
                right_now[pl.ds(i * FAM, FAM), :]
                - share_now[i]
                - GEN_WEIGHT / SNPS * genomic
                - pedigree[i]
            )
            scale = jnp.broadcast_to(step_scale[pl.ds(family_first + i, 1), :], (FAM, FAM)).T
            updated = share_now[i] + scale * residual
            if it + 1 < ITERS:
                share_now[i] = updated
                halves[it + 1][family_first + i] = updated.T.astype(BF16)
            else:
                out[0, pl.ds(i * FAM, FAM), :] = updated
                out[1, pl.ds(i * FAM, FAM), :] = residual

        if it + 1 < ITERS:
            mine = halves[it + 1].at[pl.ds(family_first, 2)]
            for d in range(SNP - 1):
                remote(
                    mine,
                    mine,
                    half_sem.at[0],
                    half_sem.at[1],
                    {"snp": peer(d)},
                ).start()
            arrived(halves[it + 1].at[pl.ds(0, 14)], half_sem.at[1])

    arrived(halves[1].at[pl.ds(0, 14)], half_sem.at[0])
    for d in range(1, RSPAN + 1):

        @pl.when(animal >= d)
        def _():
            arrived(rel_vector, request_sem.at[0, d - 1])

        @pl.when(animal + d < ANIMAL)
        def _():
            for it in range(ITERS):
                arrived(rel_send.at[it, d - 1], rel_sem.at[it, 0, d - 1])

    for it in range(ITERS):
        arrived(gen_send.at[it], gen_sem.at[it, 0])

        def sent(k, carry):
            arrived(core_send.at[it, k], core_sem.at[it, 0, k])
            arrived(core_send.at[it, k], join_sem.at[it, 0, k])
            arrived(chip_recv.at[it, k], chip_sem.at[it, 0, k])
            arrived(chip_recv.at[it, k], back_sem.at[it, 0, k])
            return carry

        lax.fori_loop(0, PLANES, sent, 0)


def per_device(
    genotypes,
    allele_frequency,
    family_size,
    rel_family,
    rel_count,
    own_block,
    rel_block,
    prior_solution,
    right_side,
    step_scale,
):
    vmem = pl.BlockSpec(memory_space=pltpu.VMEM)
    smem = pl.BlockSpec(memory_space=pltpu.SMEM)
    hbm = pl.BlockSpec(memory_space=pl.ANY)
    dma = pltpu.SemaphoreType.DMA
    both = pl.pallas_call(
        kernel,
        out_shape=jax.ShapeDtypeStruct((2, SHARE, COLS), F32),
        in_specs=[hbm, vmem, smem, smem, vmem, smem, hbm, hbm, vmem, hbm, vmem],
        out_specs=vmem,
        scratch_shapes=[
            pltpu.VMEM((ROWS, WORDS), jnp.int32),
            pltpu.VMEM((PLANES, ROWS, WORDS), F8),
            pltpu.VMEM((FAMS, COLS, FAM), BF16),
            pltpu.VMEM((FAMS, COLS, FAM), BF16),
            pltpu.VMEM((PLANES, 2, COLS, HALF), F32),
            pltpu.VMEM((ITERS, PLANES, CHIPS, BAND, HALF), BF16),
            pltpu.VMEM((ITERS, PLANES, CHIPS, BAND, HALF), BF16),
            pltpu.VMEM((ITERS, PLANES, CHIPS, BAND, HALF), BF16),
            pltpu.VMEM((ITERS, PLANES, CHIPS - 1, BAND, HALF), BF16),
            pltpu.VMEM((ITERS, PLANES, 2, CHIPS, BAND, HALF), BF16),
            pltpu.VMEM((ROWS, COLS), F32),
            pltpu.VMEM((ITERS, SNP - 1, SHARE, COLS), BF16),
            pltpu.VMEM((ITERS, SNP - 1, SHARE, COLS), BF16),
            pltpu.VMEM((2, FAM, COLS), F32),
            pltpu.VMEM((2, FAM, FAM), BF16),
            pltpu.VMEM((2, FAM, FAM), BF16),
            pltpu.VMEM((SHARE, COLS), F32),
            pltpu.VMEM((ITERS, RSPAN, 2, COLS, FAM), BF16),
            pltpu.VMEM((RSPAN, 2, COLS, FAM), BF16),
            pltpu.VMEM((RSPAN, 2, COLS, FAM), BF16),
            *[pltpu.VMEM((FAMS,), jnp.int32)] * RSPAN,
            *[pltpu.SMEM((FAMS,), jnp.int32)] * RSPAN,
            pltpu.VMEM((PLANES, 1, WORDS), F32),
            dma((ROW_BLOCKS,)),
            dma((4,)),
            dma((2, RSPAN)),
            dma((ITERS, 2, PLANES)),
            dma((ITERS, 2, PLANES)),
            dma((ITERS, 2, PLANES)),
            dma((ITERS, 2, PLANES)),
            dma((ITERS, 2)),
            dma((2,)),
            dma((ITERS, 2, RSPAN)),
        ],
        compiler_params=pltpu.CompilerParams(
            collective_id=0, has_side_effects=True, vmem_limit_bytes=66 * 10**6
        ),
        name="blup",
    )(
        genotypes,
        allele_frequency.reshape(PLANES * WORDS // 128, 128),
        family_size,
        rel_family,
        rel_family,
        rel_count,
        own_block,
        rel_block,
        prior_solution,
        right_side,
        step_scale.reshape(FAMS, FAM),
    )
    return both[0], both[1]


def solution(mesh):
    in_specs = (
        P("animal", "snp"),
        P("snp"),
        P("animal"),
        P("animal"),
        P("animal"),
        P("animal", None, None),
        P("animal", None, None),
        P("animal", None),
        P("animal", None),
        P("animal"),
    )
    out_specs = (P(("animal", "snp"), None), P(("animal", "snp"), None))
    return jax.shard_map(
        per_device, mesh=mesh, in_specs=in_specs, out_specs=out_specs, check_vma=False
    )
```
